32 devices in a mesh: shot: 4 (over y, x), dom: 8 (over z, core).
Axes of the slice: x: 2, y: 2, z: 4, core: 2. Of those that a mesh axis runs over, the one named last changes fastest.
Arguments:
- velocity: float32 [256, 32, 128], P('dom'), may hold values from 1.5 to 3
- noise_field: float32 [256, 32, 128], P('dom'), may hold values from -6 to 6
- step_size: float32 [1], replicated, may hold values from 0.05 to 0.5
- field_prev: float32 [8, 256, 32, 128], P('shot', 'dom'), may hold values from -6 to 6
- field_now: float32 [8, 256, 32, 128], P('shot', 'dom'), may hold values from -6 to 6
- adjoint_next: float32 [8, 256, 32, 128], P('shot', 'dom'), may hold values from -6 to 6
- adjoint_now: float32 [8, 256, 32, 128], P('shot', 'dom'), may hold values from -6 to 6
- wavelet: float32 [8, 4], P('shot'), may hold values from -8 to 8
- source_cells: int32 [8, 8], P('shot'), may hold values from 0 to 1048575
- source_signs: int32 [8, 8], P('shot'), may hold values from 0 to 1
- record_cells: int32 [8, 256], P('shot'), may hold values from 0 to 1048575
- observed: float32 [8, 4, 256], P('shot'), may hold values from -6 to 6
Outputs:
- new_velocity: float32 [256, 32, 128], P('dom', None, 'shot')
The draws below stay inside these ranges and needn't reach their ends.
Inputs may be any that keep to these rules, and one draw needn't show every extreme that they name: `source_signs`: 0 stands for a negative sign, 1 for a positive one. `source_cells`: cells flattened as x 32 * 128 + z * 128 + y. `record_cells`: cells flattened as x 32 * 128 + z * 128 + y.
All inputs are finite; a program needn't handle non-finite values.
Results may differ from the reference program's by a relative error of at most 0.00009.
Values sent between devices are 32-bit elements; how exact they have to be, the bound alone decides.
A program may use at most 128 MiB of HBM per device.

```python
import math
import jax
import jax.numpy as jnp
from jax import lax

NZ = 32
NY = 128
STEPS = 4
NSRC = 8
NREC = 256
NX = 256
SHOTS = 8
KC = 8


def draw_noise_field(key, part):
    sample = jax.random.normal(key, (NX, NZ, NY), jnp.float32)
    return jnp.clip(sample, -5.0, 5.0)


def touch_ends(result, rng, least, largest):
    longest = result.shape.index(max(result.shape))
    spots = []
    for shift in (0, 1):
        where = [jax.random.randint(jax.random.fold_in(rng, axis), (), 0, length) for axis, length in enumerate(result.shape)]
        where[longest] = (where[longest] + shift) % result.shape[longest]
        spots.append(tuple(where))
    return result.at[spots[0]].set(least).at[spots[1]].set(largest)


def shard_levels(key, dims, pieces, smallest, top_value):
    factor_of, own = 1.0, jax.random.fold_in(key, 6)
    for dim, shards_of in pieces:
        draws = jnp.exp(jax.random.uniform(jax.random.fold_in(own, dim), (shards_of,), jnp.float32, smallest / len(pieces), top_value / len(pieces)))
        factor_of = factor_of * jnp.repeat(draws, dims[dim] // shards_of).reshape([-1 if axis == dim else 1 for axis in range(len(dims))])
    return factor_of


def centred(stream_key, extent, width, reach, cuts=(), kind=jnp.bfloat16):
    values = width * jax.random.normal(stream_key, extent, jnp.float32)
    if cuts:
        values = values * shard_levels(stream_key, extent, cuts, -0.22, 0.18)
    return jnp.clip(values, -reach, reach).astype(kind)


def setup_inputs(seed: int = 0) -> dict:
    key_of = jax.random.split(jax.random.key(seed), 13)
    return {
        "velocity": jnp.clip(1.5 + 1.5 * jax.random.uniform(key_of[0], (NX, NZ, NY), jnp.float32) ** shard_levels(key_of[0], (NX, NZ, NY), ((0, 8),), -0.2, 0.2), 1.5, 3.0),
        "noise_field": draw_noise_field(jax.random.fold_in(key_of[12], 71), 0),
        "step_size": jnp.clip(jnp.exp(jax.random.uniform(key_of[2], (1,), jnp.float32, math.log(0.05), math.log(0.5))), 0.05, 0.5),
        "field_prev": centred(key_of[3], (SHOTS, NX, NZ, NY), 1.0, 6.0, ((0, 4), (1, 8)), jnp.float32),
        "field_now": centred(key_of[4], (SHOTS, NX, NZ, NY), 1.0, 6.0, ((0, 4), (1, 8)), jnp.float32),
        "adjoint_next": centred(key_of[5], (SHOTS, NX, NZ, NY), 1.0, 6.0, ((0, 4), (1, 8)), jnp.float32),
        "adjoint_now": centred(key_of[6], (SHOTS, NX, NZ, NY), 1.0, 6.0, ((0, 4), (1, 8)), jnp.float32),
        "wavelet": centred(key_of[7], (SHOTS, STEPS), 2.0, 8.0, ((0, 4),), jnp.float32),
        "source_cells": touch_ends(jax.random.randint(key_of[8], (SHOTS, NSRC), 0, NX * NY * NZ), jax.random.fold_in(key_of[8], 1), 0, (NX * NY * NZ) - 1).astype(jnp.int32),
        "source_signs": touch_ends(jax.random.randint(key_of[9], (SHOTS, NSRC), 0, 2), jax.random.fold_in(key_of[9], 1), 0, 1).astype(jnp.int32),
        "record_cells": touch_ends(jax.random.randint(key_of[10], (SHOTS, NREC), 0, NX * NY * NZ), jax.random.fold_in(key_of[10], 1), 0, (NX * NY * NZ) - 1).astype(jnp.int32),
        "observed": centred(key_of[11], (SHOTS, STEPS, NREC), 1.0, 6.0, ((0, 4),), jnp.float32),
    }


COEFFS = (-205.0 / 72.0, 8.0 / 5.0, -1.0 / 5.0, 8.0 / 315.0, -1.0 / 560.0)
COURANT = 0.02

def stencil(padded):
    margin = 4
    rank = padded.ndim
    lengths = [padded.shape[rank - 3 + place] - 2 * margin for place in range(3)]

    def window(offsets):
        sliced = padded
        for place in range(3):
            begin = margin + offsets[place]
            sliced = lax.slice_in_dim(sliced, begin, begin + lengths[place], axis=rank - 3 + place)
        return sliced
    summed = 3.0 * COEFFS[0] * window((0, 0, 0))
    for distance in range(1, 5):
        beside_all = window((distance, 0, 0)) + window((-distance, 0, 0))
        beside_all = beside_all + window((0, distance, 0)) + window((0, -distance, 0))
        beside_all = beside_all + window((0, 0, distance)) + window((0, 0, -distance))
        summed = summed + COEFFS[distance] * beside_all
    return summed

def cosine_basis(length):
    wave_index = jnp.arange(length, dtype=jnp.int32)[:, None]
    position = jnp.arange(length, dtype=jnp.int32)[None, :]
    phase = wave_index * (2 * position + 1) % (4 * length)
    angle = math.pi / (2.0 * length) * phase.astype(jnp.float32)
    factor = jnp.where(wave_index == 0, math.sqrt(1.0 / length), math.sqrt(2.0 / length)).astype(jnp.float32)
    return factor * jnp.cos(angle)

def prior_gain(length, cutoff):
    scaled = jnp.arange(length, dtype=jnp.float32) / float(cutoff)
    return 1.0 / jnp.sqrt(1.0 + scaled)

def reference(velocity, noise_field, step_size, field_prev, field_now, adjoint_next, adjoint_now, wavelet, source_cells, source_signs, record_cells, observed):
    speed_sq = COURANT * velocity * velocity
    grid_shape = velocity.shape

    def one_shot(carry, inputs):
        prior, current, adj_later, adj_current, pulse, sources, signs, records, measured = inputs
        amplitude = (2 * signs - 1).astype(jnp.float32)
        laplacians = []
        samples = []
        for moment in range(STEPS):
            spread = stencil(jnp.pad(current, 4))
            laplacians.append(spread)
            advanced = 2.0 * current - prior + speed_sq * spread
            advanced = advanced.reshape(-1).at[sources].add(amplitude * pulse[moment]).reshape(grid_shape)
            samples.append(advanced.reshape(-1)[records])
            prior, current = (current, advanced)
        summed = jnp.zeros(grid_shape, jnp.float32)
        for moment in range(STEPS, 0, -1):
            misfit = samples[moment - 1] - measured[moment - 1]
            spread = stencil(jnp.pad(adj_current, 4))
            earlier = 2.0 * adj_current - adj_later + speed_sq * spread
            earlier = earlier.reshape(-1).at[records].add(misfit).reshape(grid_shape)
            adj_later, adj_current = (adj_current, earlier)
            summed = summed + adj_current * laplacians[moment - 1]
        return (carry + summed, None)
    start_total = jnp.zeros(grid_shape, jnp.float32)
    total = lax.scan(one_shot, start_total, (field_prev, field_now, adjoint_next, adjoint_now, wavelet, source_cells, source_signs, record_cells, observed))[0]
    gradient = 2.0 * COURANT * velocity * total
    basis = cosine_basis(NX)
    spectrum = prior_gain(NX, KC)[:, None]
    columns = NY * NZ
    highest = lax.Precision.HIGHEST
    grad_hat = jnp.dot(basis, gradient.reshape(NX, columns), precision=highest)
    noise_hat = jnp.dot(basis, noise_field.reshape(NX, columns), precision=highest)
    rate = step_size[0]
    weights = spectrum * (-0.5 * rate * spectrum * grad_hat + jnp.sqrt(rate) * noise_hat)
    update = lax.dot_general(basis, weights, (((0,), (0,)), ((), ())), precision=highest)
    return velocity + update.reshape(NX, NZ, NY)
```

```python
import functools
import math

import jax
import jax.numpy as jnp
from jax import lax
from jax.experimental import pallas as pl
from jax.experimental.pallas import tpu as pltpu
from jax.sharding import PartitionSpec as P

STEPS = 4


COEFFS = (-205.0 / 72.0, 8.0 / 5.0, -1.0 / 5.0, 8.0 / 315.0, -1.0 / 560.0)
COURANT = 0.02


MARGIN = 4
MESH = pl.DeviceIdType.MESH


def split_two(value):
    high = value.astype(jnp.bfloat16)
    low = (value - high.astype(jnp.float32)).astype(jnp.bfloat16)
    return jnp.concatenate([high, low], axis=-1)


def wave_kernel(
    doms,
    now_hbm,
    adj_hbm,
    prev_hbm,
    later_hbm,
    speed_hbm,
    pulse,
    rec_col,
    rec_lane,
    src_col,
    src_lane,
    signs,
    observed,
    out,
    ext,
    prev,
    later,
    speed,
    laps,
    spread_src,
    landed,
    pick,
    put,
    hot,
    misfit,
    total,
    load_sem,
    send_sem,
    recv_sem,
):
    shots, rows, depth, width = prev.shape
    here = lax.axis_index("dom")
    left = jnp.maximum(here - 1, 0)
    right = jnp.minimum(here + 1, doms - 1)
    has_left = here > 0
    has_right = here < doms - 1
    chunk = 8
    chunks = rows // chunk
    high_start = rows + MARGIN

    loads = [
        pltpu.make_async_copy(now_hbm, ext.at[0, :, pl.ds(MARGIN, rows)], load_sem.at[0]),
        pltpu.make_async_copy(speed_hbm, speed, load_sem.at[1]),
        pltpu.make_async_copy(prev_hbm, prev, load_sem.at[2]),
        pltpu.make_async_copy(adj_hbm, ext.at[STEPS, :, pl.ds(MARGIN, rows)], load_sem.at[3]),
        pltpu.make_async_copy(later_hbm, later, load_sem.at[4]),
    ]
    for load in loads:
        load.start()

    barrier = pltpu.get_barrier_semaphore()

    @pl.when(has_left)
    def _():
        pl.semaphore_signal(barrier, inc=1, device_id={"dom": left}, device_id_type=MESH)

    @pl.when(has_right)
    def _():
        pl.semaphore_signal(barrier, inc=1, device_id={"dom": right}, device_id_type=MESH)

    pl.semaphore_wait(barrier, has_left.astype(jnp.int32) + has_right.astype(jnp.int32))

    def halo_copies(slot, source):
        base = MARGIN if source is None else 0
        field = ext.at[slot] if source is None else source
        to_left = pltpu.make_async_remote_copy(
            src_ref=field.at[:, pl.ds(base, MARGIN)],
            dst_ref=ext.at[slot, :, pl.ds(high_start, MARGIN)],
            send_sem=send_sem.at[slot, 0],
            recv_sem=recv_sem.at[slot, 1],
            device_id={"dom": left},
            device_id_type=MESH,
        )
        to_right = pltpu.make_async_remote_copy(
            src_ref=field.at[:, pl.ds(base + rows - MARGIN, MARGIN)],
            dst_ref=ext.at[slot, :, pl.ds(0, MARGIN)],
            send_sem=send_sem.at[slot, 1],
            recv_sem=recv_sem.at[slot, 0],
            device_id={"dom": right},
            device_id_type=MESH,
        )
        return to_left, to_right

    copies = [
        halo_copies(slot, {0: now_hbm, STEPS: adj_hbm}.get(slot)) for slot in range(2 * STEPS)
    ]

    def send(slot):
        @pl.when(has_left)
        def _():
            copies[slot][0].start()

        @pl.when(has_right)
        def _():
            copies[slot][1].start()

    def receive(slot):
        @pl.when(has_left)
        def _():
            copies[slot][1].wait_recv()

        @pl.when(has_right)
        def _():
            copies[slot][0].wait_recv()

    send(0)
    send(STEPS)

    edge = jnp.zeros((2 * STEPS, shots, MARGIN, depth, width), jnp.float32)

    @pl.when(jnp.logical_not(has_left))
    def _():
        ext[pl.ds(0, 2 * STEPS), :, pl.ds(0, MARGIN)] = edge

    @pl.when(jnp.logical_not(has_right))
    def _():
        ext[pl.ds(0, 2 * STEPS), :, pl.ds(high_start, MARGIN)] = edge

    lanes = lax.broadcasted_iota(jnp.int32, (depth, width), 1)
    levels = lax.broadcasted_iota(jnp.int32, (depth, width), 0)

    span = chunk * depth
    receivers = rec_lane.shape[2]
    sources = src_lane.shape[2]
    for s in range(shots):
        hot[s] = (
            lax.broadcasted_iota(jnp.int32, (receivers, width), 1) == rec_col[s, :, 1:2]
        ).astype(jnp.float32)
        tall = (
            lax.broadcasted_iota(jnp.int32, (sources, width), 1) == src_col[s]
        ).astype(jnp.float32) * signs[s]
        tall = tall.astype(jnp.bfloat16)

        @pl.loop(0, chunks)
        def _(c):
            cell = lax.broadcasted_iota(jnp.int32, (receivers, span), 1) + c * span
            pick[s, c] = (cell == rec_col[s, :, 0:1]).astype(jnp.float32).astype(jnp.bfloat16)
            cell = lax.broadcasted_iota(jnp.int32, (span, receivers), 0) + c * span
            put[s, c] = (cell == rec_lane[s]).astype(jnp.float32).astype(jnp.bfloat16)
            cell = lax.broadcasted_iota(jnp.int32, (span, sources), 0) + c * span
            wide = (cell == src_lane[s]).astype(jnp.float32).astype(jnp.bfloat16)
            spots = jnp.dot(wide, tall, preferred_element_type=jnp.float32)
            spread_src[s, pl.ds(c * chunk, chunk)] = spots.reshape(chunk, depth, width)

    def laplacian(slot, s, x):
        middle = ext[slot, s, x + MARGIN]
        summed = 3.0 * COEFFS[0] * middle
        for r in range(1, MARGIN + 1):
            beside = ext[slot, s, x + MARGIN + r] + ext[slot, s, x + MARGIN - r]
            beside += jnp.where(levels < depth - r, pltpu.roll(middle, depth - r, 0), 0.0)
            beside += jnp.where(levels >= r, pltpu.roll(middle, r, 0), 0.0)
            beside += jnp.where(lanes < width - r, pltpu.roll(middle, width - r, 1), 0.0)
            beside += jnp.where(lanes >= r, pltpu.roll(middle, r, 1), 0.0)
            summed += COEFFS[r] * beside
        return middle, summed

    def forward(moment, first, last):
        @pl.loop(first, last)
        def _(x):
            squared = COURANT * speed[x] * speed[x]
            for s in range(shots):
                middle, summed = laplacian(moment, s, x)
                before = prev[s, x] if moment == 0 else ext[moment - 1, s, x + MARGIN]
                laps[moment, s, x] = summed
                slot = moment + 1 if moment + 1 < STEPS else 2 * STEPS
                ext[slot, s, x + MARGIN] = (
                    2.0 * middle - before + squared * summed + pulse[s, moment] * spread_src[s, x]
                )

    def backward(moment, first, last):
        slot = 2 * STEPS - moment

        @pl.loop(first, last)
        def _(x):
            squared = COURANT * speed[x] * speed[x]
            gathered = None
            for s in range(shots):
                middle, summed = laplacian(slot, s, x)
                after = later[s, x] if moment == STEPS else ext[slot - 1, s, x + MARGIN]
                earlier = 2.0 * middle - after + squared * summed + landed[moment - 1, s, x]
                if moment > 1:
                    ext[slot + 1, s, x + MARGIN] = earlier
                term = earlier * laps[moment - 1, s, x]
                gathered = term if gathered is None else gathered + term
            if moment < STEPS:
                gathered = gathered + total[x]
            if moment > 1:
                total[x] = gathered
            else:
                out[x] = 2.0 * COURANT * speed[x] * gathered

    def receivers_at(moment):
        slot = moment if moment < STEPS else 2 * STEPS
        for s in range(shots):
            @pl.loop(0, chunks)
            def _(c):
                block = ext[slot, s, pl.ds(MARGIN + c * chunk, chunk)].reshape(span, width)
                part = jnp.dot(pick[s, c], split_two(block), preferred_element_type=jnp.float32)

                @pl.when(c == 0)
                def _():
                    misfit[...] = part

                @pl.when(c > 0)
                def _():
                    misfit[...] += part

            found = misfit[:, :width] + misfit[:, width:]
            sample = jnp.sum(found * hot[s], axis=1, keepdims=True)
            miss = sample - observed[s, :, moment - 1 : moment]
            values = split_two(miss * hot[s])

            @pl.loop(0, chunks)
            def _(c):
                both = jnp.dot(put[s, c], values, preferred_element_type=jnp.float32)
                landed[moment - 1, s, pl.ds(c * chunk, chunk)] = (
                    both[:, :width] + both[:, width:]
                ).reshape(chunk, depth, width)

    for load in loads[:3]:
        load.wait()
    forward(0, MARGIN, rows - MARGIN)
    receive(0)
    forward(0, 0, MARGIN)
    forward(0, rows - MARGIN, rows)
    send(1)
    receivers_at(1)
    for moment in range(1, STEPS):
        receive(moment)
        forward(moment, 0, MARGIN)
        forward(moment, rows - MARGIN, rows)
        if moment + 1 < STEPS:
            send(moment + 1)
        forward(moment, MARGIN, rows - MARGIN)
        receivers_at(moment + 1)
    for load in loads[3:]:
        load.wait()
    for moment in range(STEPS, 0, -1):
        slot = 2 * STEPS - moment
        receive(slot)
        backward(moment, 0, MARGIN)
        backward(moment, rows - MARGIN, rows)
        if moment > 1:
            send(slot + 1)
        backward(moment, MARGIN, rows - MARGIN)
    for slot in range(2 * STEPS):
        @pl.when(has_left)
        def _():
            copies[slot][0].wait_send()

        @pl.when(has_right)
        def _():
            copies[slot][1].wait_send()


def shot_gradient(
    velocity, prev, now, later, adjoint, wavelet, source_cells, signs, record_cells, observed
):
    shots, rows, depth, width = now.shape
    first = lax.axis_index("dom") * rows * depth
    receivers = record_cells.shape[1]
    padding = (-source_cells.shape[1]) % 128
    pad = ((0, 0), (0, padding))
    rec_rows = record_cells // width - first
    rec_col = jnp.stack([rec_rows, record_cells % width], axis=-1)
    src_rows = jnp.pad(source_cells // width - first, pad, constant_values=-1)
    src_lanes = jnp.pad(source_cells % width, pad)
    amplitude = jnp.pad((2 * signs - 1).astype(jnp.float32), pad)
    count = src_rows.shape[1]
    chunk = 8
    span = chunk * depth
    hbm = pl.BlockSpec(memory_space=pl.ANY)
    vmem = pl.BlockSpec(memory_space=pltpu.VMEM)
    smem = pl.BlockSpec(memory_space=pltpu.SMEM)
    f32 = jnp.float32
    return pl.pallas_call(
        functools.partial(wave_kernel, lax.axis_size("dom")),
        out_shape=jax.ShapeDtypeStruct((rows, depth, width), f32),
        in_specs=[hbm] * 5 + [smem] + [vmem] * 6,
        out_specs=vmem,
        scratch_shapes=[
            pltpu.VMEM((2 * STEPS + 1, shots, rows + 2 * MARGIN, depth, width), f32),
            pltpu.VMEM((shots, rows, depth, width), f32),
            pltpu.VMEM((shots, rows, depth, width), f32),
            pltpu.VMEM((rows, depth, width), f32),
            pltpu.VMEM((STEPS, shots, rows, depth, width), f32),
            pltpu.VMEM((shots, rows, depth, width), f32),
            pltpu.VMEM((STEPS, shots, rows, depth, width), f32),
            pltpu.VMEM((shots, rows // chunk, receivers, span), jnp.bfloat16),
            pltpu.VMEM((shots, rows // chunk, span, receivers), jnp.bfloat16),
            pltpu.VMEM((shots, receivers, width), f32),
            pltpu.VMEM((receivers, 2 * width), f32),
            pltpu.VMEM((rows, depth, width), f32),
            pltpu.SemaphoreType.DMA((5,)),
            pltpu.SemaphoreType.DMA((2 * STEPS, 2)),
            pltpu.SemaphoreType.DMA((2 * STEPS, 2)),
        ],
        compiler_params=pltpu.CompilerParams(
            collective_id=0, has_side_effects=True, vmem_limit_bytes=56 * 1024 * 1024
        ),
    )(
        now,
        adjoint,
        prev,
        later,
        velocity,
        wavelet,
        rec_col,
        rec_rows[:, None, :],
        src_lanes[:, :, None],
        src_rows[:, None, :],
        amplitude[:, :, None],
        jnp.swapaxes(observed, 1, 2),
    )


def cosine_basis(length):
    wave_index = jnp.arange(length, dtype=jnp.int32)[:, None]
    position = jnp.arange(length, dtype=jnp.int32)[None, :]
    phase = wave_index * (2 * position + 1) % (4 * length)
    angle = math.pi / (2.0 * length) * phase.astype(jnp.float32)
    factor = jnp.where(wave_index == 0, math.sqrt(1.0 / length), math.sqrt(2.0 / length)).astype(
        jnp.float32
    )
    return factor * jnp.cos(angle)


def prior_gain(length, cutoff):
    scaled = jnp.arange(length, dtype=jnp.float32) / float(cutoff)
    return 1.0 / jnp.sqrt(1.0 + scaled)


def precondition(gradient, noise_cols, rate):
    length = gradient.shape[0]
    basis = cosine_basis(length)
    spectrum = prior_gain(length, length // 32)[:, None]
    highest = lax.Precision.HIGHEST
    grad_hat = jnp.dot(basis, gradient.reshape(length, -1), precision=highest)
    noise_hat = jnp.dot(basis, noise_cols.reshape(length, -1), precision=highest)
    weights = spectrum * (-0.5 * rate * spectrum * grad_hat + jnp.sqrt(rate) * noise_hat)
    update = lax.dot_general(basis, weights, (((0,), (0,)), ((), ())), precision=highest)
    return update.reshape(gradient.shape)


def body(
    velocity,
    noise_field,
    step_size,
    field_prev,
    field_now,
    adjoint_next,
    adjoint_now,
    wavelet,
    source_cells,
    source_signs,
    record_cells,
    observed,
):
    partial_value = shot_gradient(
        velocity,
        field_prev,
        field_now,
        adjoint_next,
        adjoint_now,
        wavelet,
        source_cells,
        source_signs,
        record_cells,
        observed,
    )
    rate = step_size[0]
    shot_rows = velocity.shape[2] // lax.axis_size("shot")
    start = lax.axis_index("shot") * shot_rows
    share = lax.psum_scatter(partial_value, "shot", scatter_dimension=2, tiled=True)
    noise_part = lax.dynamic_slice_in_dim(noise_field, start, shot_rows, 2)
    grad_cols, noise_cols = (
        lax.all_to_all(share, "dom", split_axis=2, concat_axis=0, tiled=True),
        lax.all_to_all(noise_part, "dom", split_axis=2, concat_axis=0, tiled=True),
    )
    update = precondition(grad_cols, noise_cols, rate)
    returned = lax.all_to_all(update, "dom", split_axis=0, concat_axis=2, tiled=True)
    result = lax.dynamic_slice_in_dim(velocity, start, shot_rows, 2) + returned
    return result


def solution(mesh):
    placed = (
        P("dom", None, None),
        P("dom", None, None),
        P(),
        P("shot", "dom", None, None),
        P("shot", "dom", None, None),
        P("shot", "dom", None, None),
        P("shot", "dom", None, None),
        P("shot", None),
        P("shot", None),
        P("shot", None),
        P("shot", None),
        P("shot", None, None),
    )
    return jax.shard_map(
        body, mesh=mesh, in_specs=placed, out_specs=P("dom", None, "shot"), check_vma=False
    )
```

```python
import functools
import math

import jax
import jax.numpy as jnp
import numpy as np
from jax import lax
from jax.experimental import pallas as pl
from jax.experimental.pallas import tpu as pltpu
from jax.sharding import PartitionSpec as P

STEPS = 4


COEFFS = (-205.0 / 72.0, 8.0 / 5.0, -1.0 / 5.0, 8.0 / 315.0, -1.0 / 560.0)
COURANT = 0.02


MARGIN = 4
MESH = pl.DeviceIdType.MESH


def split_two(value):
    high = value.astype(jnp.bfloat16)
    low = (value - high.astype(jnp.float32)).astype(jnp.bfloat16)
    return jnp.concatenate([high, low], axis=-1)


def wave_kernel(
    doms,
    now_hbm,
    adj_hbm,
    prev_hbm,
    later_hbm,
    speed_hbm,
    pulse,
    rec_col,
    rec_lane,
    src_col,
    src_lane,
    signs,
    observed,
    out,
    ext,
    prev,
    later,
    speed,
    laps,
    spread_src,
    landed,
    pick,
    put,
    hot,
    misfit,
    total,
    load_sem,
    send_sem,
    recv_sem,
):
    shots, rows, depth, width = prev.shape
    here = lax.axis_index("dom")
    left = jnp.maximum(here - 1, 0)
    right = jnp.minimum(here + 1, doms - 1)
    has_left = here > 0
    has_right = here < doms - 1
    chunk = 8
    chunks = rows // chunk
    high_start = rows + MARGIN

    loads = [
        pltpu.make_async_copy(now_hbm, ext.at[0, :, pl.ds(MARGIN, rows)], load_sem.at[0]),
        pltpu.make_async_copy(speed_hbm, speed, load_sem.at[1]),
        pltpu.make_async_copy(prev_hbm, prev, load_sem.at[2]),
        pltpu.make_async_copy(adj_hbm, ext.at[STEPS, :, pl.ds(MARGIN, rows)], load_sem.at[3]),
        pltpu.make_async_copy(later_hbm, later, load_sem.at[4]),
    ]
    for load in loads:
        load.start()

    barrier = pltpu.get_barrier_semaphore()

    @pl.when(has_left)
    def _():
        pl.semaphore_signal(barrier, inc=1, device_id={"dom": left}, device_id_type=MESH)

    @pl.when(has_right)
    def _():
        pl.semaphore_signal(barrier, inc=1, device_id={"dom": right}, device_id_type=MESH)

    pl.semaphore_wait(barrier, has_left.astype(jnp.int32) + has_right.astype(jnp.int32))

    def halo_copies(slot, source):
        base = MARGIN if source is None else 0
        field = ext.at[slot] if source is None else source
        to_left = pltpu.make_async_remote_copy(
            src_ref=field.at[:, pl.ds(base, MARGIN)],
            dst_ref=ext.at[slot, :, pl.ds(high_start, MARGIN)],
            send_sem=send_sem.at[slot, 0],
            recv_sem=recv_sem.at[slot, 1],
            device_id={"dom": left},
            device_id_type=MESH,
        )
        to_right = pltpu.make_async_remote_copy(
            src_ref=field.at[:, pl.ds(base + rows - MARGIN, MARGIN)],
            dst_ref=ext.at[slot, :, pl.ds(0, MARGIN)],
            send_sem=send_sem.at[slot, 1],
            recv_sem=recv_sem.at[slot, 0],
            device_id={"dom": right},
            device_id_type=MESH,
        )
        return to_left, to_right

    copies = [
        halo_copies(slot, {0: now_hbm, STEPS: adj_hbm}.get(slot)) for slot in range(2 * STEPS)
    ]

    def send(slot):
        @pl.when(has_left)
        def _():
            copies[slot][0].start()

        @pl.when(has_right)
        def _():
            copies[slot][1].start()

    def receive(slot):
        @pl.when(has_left)
        def _():
            copies[slot][1].wait_recv()

        @pl.when(has_right)
        def _():
            copies[slot][0].wait_recv()

    send(0)
    send(STEPS)

    edge = jnp.zeros((2 * STEPS, shots, MARGIN, depth, width), jnp.float32)

    @pl.when(jnp.logical_not(has_left))
    def _():
        ext[pl.ds(0, 2 * STEPS), :, pl.ds(0, MARGIN)] = edge

    @pl.when(jnp.logical_not(has_right))
    def _():
        ext[pl.ds(0, 2 * STEPS), :, pl.ds(high_start, MARGIN)] = edge

    lanes = lax.broadcasted_iota(jnp.int32, (depth, width), 1)
    levels = lax.broadcasted_iota(jnp.int32, (depth, width), 0)

    span = chunk * depth
    receivers = rec_lane.shape[2]
    sources = src_lane.shape[2]
    for s in range(shots):
        hot[s] = (
            lax.broadcasted_iota(jnp.int32, (receivers, width), 1) == rec_col[s, :, 1:2]
        ).astype(jnp.float32)
        tall = (
            lax.broadcasted_iota(jnp.int32, (sources, width), 1) == src_col[s]
        ).astype(jnp.float32) * signs[s]
        tall = tall.astype(jnp.bfloat16)

        @pl.loop(0, chunks)
        def _(c):
            cell = lax.broadcasted_iota(jnp.int32, (receivers, span), 1) + c * span
            pick[s, c] = (cell == rec_col[s, :, 0:1]).astype(jnp.float32).astype(jnp.bfloat16)
            cell = lax.broadcasted_iota(jnp.int32, (span, receivers), 0) + c * span
            put[s, c] = (cell == rec_lane[s]).astype(jnp.float32).astype(jnp.bfloat16)
            cell = lax.broadcasted_iota(jnp.int32, (span, sources), 0) + c * span
            wide = (cell == src_lane[s]).astype(jnp.float32).astype(jnp.bfloat16)
            spots = jnp.dot(wide, tall, preferred_element_type=jnp.float32)
            spread_src[s, pl.ds(c * chunk, chunk)] = spots.reshape(chunk, depth, width)

    def laplacian(slot, s, x):
        middle = ext[slot, s, x + MARGIN]
        summed = 3.0 * COEFFS[0] * middle
        for r in range(1, MARGIN + 1):
            beside = ext[slot, s, x + MARGIN + r] + ext[slot, s, x + MARGIN - r]
            beside += jnp.where(levels < depth - r, pltpu.roll(middle, depth - r, 0), 0.0)
            beside += jnp.where(levels >= r, pltpu.roll(middle, r, 0), 0.0)
            beside += jnp.where(lanes < width - r, pltpu.roll(middle, width - r, 1), 0.0)
            beside += jnp.where(lanes >= r, pltpu.roll(middle, r, 1), 0.0)
            summed += COEFFS[r] * beside
        return middle, summed

    def forward(moment, first, last):
        @pl.loop(first, last)
        def _(x):
            squared = COURANT * speed[x] * speed[x]
            for s in range(shots):
                middle, summed = laplacian(moment, s, x)
                before = prev[s, x] if moment == 0 else ext[moment - 1, s, x + MARGIN]
                laps[moment, s, x] = summed
                slot = moment + 1 if moment + 1 < STEPS else 2 * STEPS
                ext[slot, s, x + MARGIN] = (
                    2.0 * middle - before + squared * summed + pulse[s, moment] * spread_src[s, x]
                )

    def backward(moment, first, last):
        slot = 2 * STEPS - moment

        @pl.loop(first, last)
        def _(x):
            squared = COURANT * speed[x] * speed[x]
            gathered = None
            for s in range(shots):
                middle, summed = laplacian(slot, s, x)
                after = later[s, x] if moment == STEPS else ext[slot - 1, s, x + MARGIN]
                earlier = 2.0 * middle - after + squared * summed + landed[moment - 1, s, x]
                if moment > 1:
                    ext[slot + 1, s, x + MARGIN] = earlier
                term = earlier * laps[moment - 1, s, x]
                gathered = term if gathered is None else gathered + term
            if moment < STEPS:
                gathered = gathered + total[x]
            if moment > 1:
                total[x] = gathered
            else:
                out[x] = 2.0 * COURANT * speed[x] * gathered

    def receivers_at(moment):
        slot = moment if moment < STEPS else 2 * STEPS
        for s in range(shots):
            @pl.loop(0, chunks)
            def _(c):
                block = ext[slot, s, pl.ds(MARGIN + c * chunk, chunk)].reshape(span, width)
                part = jnp.dot(pick[s, c], split_two(block), preferred_element_type=jnp.float32)

                @pl.when(c == 0)
                def _():
                    misfit[...] = part

                @pl.when(c > 0)
                def _():
                    misfit[...] += part

            found = misfit[:, :width] + misfit[:, width:]
            sample = jnp.sum(found * hot[s], axis=1, keepdims=True)
            miss = sample - observed[s, :, moment - 1 : moment]
            values = split_two(miss * hot[s])

            @pl.loop(0, chunks)
            def _(c):
                both = jnp.dot(put[s, c], values, preferred_element_type=jnp.float32)
                landed[moment - 1, s, pl.ds(c * chunk, chunk)] = (
                    both[:, :width] + both[:, width:]
                ).reshape(chunk, depth, width)

    for load in loads[:3]:
        load.wait()
    forward(0, MARGIN, rows - MARGIN)
    receive(0)
    forward(0, 0, MARGIN)
    forward(0, rows - MARGIN, rows)
    send(1)
    receivers_at(1)
    for moment in range(1, STEPS):
        receive(moment)
        forward(moment, 0, MARGIN)
        forward(moment, rows - MARGIN, rows)
        if moment + 1 < STEPS:
            send(moment + 1)
        forward(moment, MARGIN, rows - MARGIN)
        receivers_at(moment + 1)
    for load in loads[3:]:
        load.wait()
    for moment in range(STEPS, 0, -1):
        slot = 2 * STEPS - moment
        receive(slot)
        backward(moment, 0, MARGIN)
        backward(moment, rows - MARGIN, rows)
        if moment > 1:
            send(slot + 1)
        backward(moment, MARGIN, rows - MARGIN)
    for slot in range(2 * STEPS):
        @pl.when(has_left)
        def _():
            copies[slot][0].wait_send()

        @pl.when(has_right)
        def _():
            copies[slot][1].wait_send()


def shot_gradient(
    velocity, prev, now, later, adjoint, wavelet, source_cells, signs, record_cells, observed
):
    shots, rows, depth, width = now.shape
    first = lax.axis_index("dom") * rows * depth
    receivers = record_cells.shape[1]
    padding = (-source_cells.shape[1]) % 128
    pad = ((0, 0), (0, padding))
    rec_rows = record_cells // width - first
    rec_col = jnp.stack([rec_rows, record_cells % width], axis=-1)
    src_rows = jnp.pad(source_cells // width - first, pad, constant_values=-1)
    src_lanes = jnp.pad(source_cells % width, pad)
    amplitude = jnp.pad((2 * signs - 1).astype(jnp.float32), pad)
    count = src_rows.shape[1]
    chunk = 8
    span = chunk * depth
    hbm = pl.BlockSpec(memory_space=pl.ANY)
    vmem = pl.BlockSpec(memory_space=pltpu.VMEM)
    smem = pl.BlockSpec(memory_space=pltpu.SMEM)
    f32 = jnp.float32
    return pl.pallas_call(
        functools.partial(wave_kernel, lax.axis_size("dom")),
        out_shape=jax.ShapeDtypeStruct((rows, depth, width), f32),
        in_specs=[hbm] * 5 + [smem] + [vmem] * 6,
        out_specs=vmem,
        scratch_shapes=[
            pltpu.VMEM((2 * STEPS + 1, shots, rows + 2 * MARGIN, depth, width), f32),
            pltpu.VMEM((shots, rows, depth, width), f32),
            pltpu.VMEM((shots, rows, depth, width), f32),
            pltpu.VMEM((rows, depth, width), f32),
            pltpu.VMEM((STEPS, shots, rows, depth, width), f32),
            pltpu.VMEM((shots, rows, depth, width), f32),
            pltpu.VMEM((STEPS, shots, rows, depth, width), f32),
            pltpu.VMEM((shots, rows // chunk, receivers, span), jnp.bfloat16),
            pltpu.VMEM((shots, rows // chunk, span, receivers), jnp.bfloat16),
            pltpu.VMEM((shots, receivers, width), f32),
            pltpu.VMEM((receivers, 2 * width), f32),
            pltpu.VMEM((rows, depth, width), f32),
            pltpu.SemaphoreType.DMA((5,)),
            pltpu.SemaphoreType.DMA((2 * STEPS, 2)),
            pltpu.SemaphoreType.DMA((2 * STEPS, 2)),
        ],
        compiler_params=pltpu.CompilerParams(
            collective_id=0, has_side_effects=True, vmem_limit_bytes=56 * 1024 * 1024
        ),
    )(
        now,
        adjoint,
        prev,
        later,
        velocity,
        wavelet,
        rec_col,
        rec_rows[:, None, :],
        src_lanes[:, :, None],
        src_rows[:, None, :],
        amplitude[:, :, None],
        jnp.swapaxes(observed, 1, 2),
    )


def cosine_basis(length):
    wave_index = jnp.arange(length, dtype=jnp.int32)[:, None]
    position = jnp.arange(length, dtype=jnp.int32)[None, :]
    phase = wave_index * (2 * position + 1) % (4 * length)
    angle = math.pi / (2.0 * length) * phase.astype(jnp.float32)
    factor = jnp.where(wave_index == 0, math.sqrt(1.0 / length), math.sqrt(2.0 / length)).astype(
        jnp.float32
    )
    return factor * jnp.cos(angle)


def prior_gain(length, cutoff):
    scaled = jnp.arange(length, dtype=jnp.float32) / float(cutoff)
    return 1.0 / jnp.sqrt(1.0 + scaled)


def precondition(gradient, noise_cols, rate):
    length = gradient.shape[0]
    basis = cosine_basis(length)
    spectrum = prior_gain(length, length // 32)[:, None]
    highest = lax.Precision.HIGHEST
    grad_hat = jnp.dot(basis, gradient.reshape(length, -1), precision=highest)
    noise_hat = jnp.dot(basis, noise_cols.reshape(length, -1), precision=highest)
    weights = spectrum * (-0.5 * rate * spectrum * grad_hat + jnp.sqrt(rate) * noise_hat)
    update = lax.dot_general(basis, weights, (((0,), (0,)), ((), ())), precision=highest)
    return update.reshape(gradient.shape)


def shared_kernel(
    shots,
    doms,
    partial,
    noise,
    basis,
    basis_t,
    gain,
    step_size,
    out,
    folded,
    noise_fold,
    sums,
    own,
    noise_lines,
    grad_lines,
    update,
    returned,
    send_sem,
    recv_sem,
    shot_send,
    shot_recv,
):
    depth, rows, width = shots * folded.shape[1], folded.shape[2], folded.shape[3]
    fold = folded.shape[1]
    lot = fold // doms
    lane_share = width // shots
    me = lax.axis_index("shot")
    here = lax.axis_index("dom")
    dom_peer = [lax.rem(here + o, doms) for o in range(doms)]
    shot_peer = [lax.rem(me + o, shots) for o in range(shots)]

    barrier = pltpu.get_barrier_semaphore()
    for o in range(1, doms):
        pl.semaphore_signal(barrier, inc=1, device_id={"dom": dom_peer[o]}, device_id_type=MESH)
    for o in range(1, shots):
        pl.semaphore_signal(barrier, inc=1, device_id={"shot": shot_peer[o]}, device_id_type=MESH)

    group = lax.broadcasted_iota(jnp.int32, (rows, width), 1) // lane_share

    def fold_lanes(source, target):
        @pl.loop(0, fold)
        def _(level):
            slabs = [
                source[pl.ds(block * fold + level, rows, stride=depth), :]
                for block in range(shots)
            ]
            for share in range(shots):
                merged = None
                for block in range(shots):
                    shift = (block - share) * lane_share % width
                    turned = pltpu.roll(slabs[block], shift, 1) if shift else slabs[block]
                    merged = turned if merged is None else jnp.where(group == block, turned, merged)
                target[share, level] = merged

    def exchange(phase, source_of, target):
        moves = []
        for o in range(1, doms):
            moves.append(
                pltpu.make_async_remote_copy(
                    src_ref=source_of(dom_peer[o]),
                    dst_ref=target.at[here],
                    send_sem=send_sem.at[phase, o],
                    recv_sem=recv_sem.at[phase, o],
                    device_id={"dom": dom_peer[o]},
                    device_id_type=MESH,
                )
            )
        return moves

    fold_lanes(partial, folded)
    pl.semaphore_wait(barrier, doms + shots - 2)
    sharing = []
    for o in range(1, shots):
        move = pltpu.make_async_remote_copy(
            src_ref=folded.at[shot_peer[o]],
            dst_ref=sums.at[o],
            send_sem=shot_send.at[o],
            recv_sem=shot_recv.at[o],
            device_id={"shot": shot_peer[o]},
            device_id_type=MESH,
        )
        move.start()
        sharing.append(move)
    fold_lanes(noise, noise_fold)
    noise_moves = exchange(0, lambda d: noise_fold.at[me, pl.ds(d * lot, lot)], noise_lines)
    for move in noise_moves:
        move.start()
    noise_lines[here] = noise_fold[me, pl.ds(here * lot, lot)]
    for move in noise_moves:
        move.wait_recv()
    rate = step_size[0]
    highest = lax.Precision.HIGHEST
    lines = doms * rows
    noise_hats = [
        jnp.dot(
            basis[...],
            noise_lines[:, i].reshape(lines, width),
            precision=highest,
            preferred_element_type=jnp.float32,
        )
        for i in range(lot)
    ]
    root = jnp.sqrt(jnp.full((1, 1), rate, jnp.float32))
    for move in sharing:
        move.wait_recv()
    gathered = folded[me]
    for o in range(1, shots):
        gathered = gathered + sums[o]
    own[...] = gathered
    grad_moves = exchange(1, lambda d: own.at[pl.ds(d * lot, lot)], grad_lines)
    for move in grad_moves:
        move.start()
    grad_lines[here] = own[pl.ds(here * lot, lot)]
    for move in grad_moves:
        move.wait_recv()
    for i in range(lot):
        grad_hat = jnp.dot(
            basis[...],
            grad_lines[:, i].reshape(lines, width),
            precision=highest,
            preferred_element_type=jnp.float32,
        )
        weights = gain[...] * (-0.5 * rate * gain[...] * grad_hat + root * noise_hats[i])
        update[:, i] = jnp.dot(
            basis_t[...], weights, precision=highest, preferred_element_type=jnp.float32
        ).reshape(doms, rows, width)
    back_moves = exchange(2, lambda d: update.at[d], returned)
    for move in back_moves:
        move.start()
    returned[here] = update[here]
    for move in back_moves:
        move.wait_recv()
    for d in range(doms):
        for i in range(lot):
            line = returned[d, i]
            for block in range(shots):
                shift = -block * lane_share % width
                turned = pltpu.roll(line, shift, 1) if shift else line
                out[pl.ds(block * fold + d * lot + i, rows, stride=depth), :] = turned
    for move in sharing + noise_moves + grad_moves + back_moves:
        move.wait_send()


def shared_update(partial_value, noise_field, step_size):
    rows, depth, width = partial_value.shape
    shots, doms = lax.axis_size("shot"), lax.axis_size("dom")
    length = rows * doms
    fold = depth // shots
    lot = fold // doms
    wave = np.arange(length)[:, None]
    phase = wave * (2 * np.arange(length)[None, :] + 1) % (4 * length)
    factor = np.where(wave == 0, math.sqrt(1.0 / length), math.sqrt(2.0 / length))
    basis = (factor * np.cos(math.pi / (2.0 * length) * phase)).astype(np.float32)
    gain = (1.0 / np.sqrt(1.0 + wave / (length // 32))).astype(np.float32)
    f32 = jnp.float32
    vmem = pl.BlockSpec(memory_space=pltpu.VMEM)
    smem = pl.BlockSpec(memory_space=pltpu.SMEM)
    result = pl.pallas_call(
        functools.partial(shared_kernel, shots, doms),
        out_shape=jax.ShapeDtypeStruct((rows * depth, width), f32),
        in_specs=[vmem] * 5 + [smem],
        out_specs=vmem,
        scratch_shapes=[
            pltpu.VMEM((shots, fold, rows, width), f32),
            pltpu.VMEM((shots, fold, rows, width), f32),
            pltpu.VMEM((shots, fold, rows, width), f32),
            pltpu.VMEM((fold, rows, width), f32),
            pltpu.VMEM((doms, lot, rows, width), f32),
            pltpu.VMEM((doms, lot, rows, width), f32),
            pltpu.VMEM((doms, lot, rows, width), f32),
            pltpu.VMEM((doms, lot, rows, width), f32),
            pltpu.SemaphoreType.DMA((3, doms)),
            pltpu.SemaphoreType.DMA((3, doms)),
            pltpu.SemaphoreType.DMA((shots,)),
            pltpu.SemaphoreType.DMA((shots,)),
        ],
        compiler_params=pltpu.CompilerParams(
            collective_id=1, has_side_effects=True, vmem_limit_bytes=32 * 1024 * 1024
        ),
    )(
        partial_value.reshape(rows * depth, width),
        noise_field.reshape(rows * depth, width),
        jnp.asarray(basis),
        jnp.asarray(np.ascontiguousarray(basis.T)),
        jnp.asarray(gain),
        step_size,
    )
    return result.reshape(rows, depth, width)[:, :, : width // shots]


def body(
    velocity,
    noise_field,
    step_size,
    field_prev,
    field_now,
    adjoint_next,
    adjoint_now,
    wavelet,
    source_cells,
    source_signs,
    record_cells,
    observed,
):
    partial_value = shot_gradient(
        velocity,
        field_prev,
        field_now,
        adjoint_next,
        adjoint_now,
        wavelet,
        source_cells,
        source_signs,
        record_cells,
        observed,
    )
    rate = step_size[0]
    shot_rows = velocity.shape[2] // lax.axis_size("shot")
    start = lax.axis_index("shot") * shot_rows
    if velocity.shape[1] % (lax.axis_size("shot") * lax.axis_size("dom")) == 0:
        moved = shared_update(partial_value, noise_field, step_size)
        return lax.dynamic_slice_in_dim(velocity, start, shot_rows, 2) + moved
    share = lax.psum_scatter(partial_value, "shot", scatter_dimension=2, tiled=True)
    noise_part = lax.dynamic_slice_in_dim(noise_field, start, shot_rows, 2)
    grad_cols, noise_cols = (
        lax.all_to_all(share, "dom", split_axis=2, concat_axis=0, tiled=True),
        lax.all_to_all(noise_part, "dom", split_axis=2, concat_axis=0, tiled=True),
    )
    update = precondition(grad_cols, noise_cols, rate)
    returned = lax.all_to_all(update, "dom", split_axis=0, concat_axis=2, tiled=True)
    result = lax.dynamic_slice_in_dim(velocity, start, shot_rows, 2) + returned
    return result


def solution(mesh):
    placed = (
        P("dom", None, None),
        P("dom", None, None),
        P(),
        P("shot", "dom", None, None),
        P("shot", "dom", None, None),
        P("shot", "dom", None, None),
        P("shot", "dom", None, None),
        P("shot", None),
        P("shot", None),
        P("shot", None),
        P("shot", None),
        P("shot", None, None),
    )
    return jax.shard_map(
        body, mesh=mesh, in_specs=placed, out_specs=P("dom", None, "shot"), check_vma=False
    )
```

```python
import functools
import math

import jax
import jax.numpy as jnp
import numpy as np
from jax import lax
from jax.experimental import pallas as pl
from jax.experimental.pallas import tpu as pltpu
from jax.sharding import PartitionSpec as P

STEPS = 4


COEFFS = (-205.0 / 72.0, 8.0 / 5.0, -1.0 / 5.0, 8.0 / 315.0, -1.0 / 560.0)
COURANT = 0.02


MARGIN = 4
MESH = pl.DeviceIdType.MESH


def split_two(value):
    high = value.astype(jnp.bfloat16)
    low = (value - high.astype(jnp.float32)).astype(jnp.bfloat16)
    return jnp.concatenate([high, low], axis=-1)


def wave_kernel(
    doms,
    now_hbm,
    adj_hbm,
    prev_hbm,
    later_hbm,
    speed_hbm,
    pulse,
    src_cells,
    src_signs,
    record_cells,
    observed,
    out,
    ext,
    prev,
    later,
    speed,
    laps,
    spread_src,
    landed,
    pick,
    put,
    hot,
    columns,
    misfit,
    total,
    load_sem,
    send_sem,
    recv_sem,
):
    shots, rows, depth, width = prev.shape
    here = lax.axis_index("dom")
    left = jnp.maximum(here - 1, 0)
    right = jnp.minimum(here + 1, doms - 1)
    has_left = here > 0
    has_right = here < doms - 1
    chunk = 8
    chunks = rows // chunk
    high_start = rows + MARGIN

    loads = [
        pltpu.make_async_copy(now_hbm, ext.at[0, :, pl.ds(MARGIN, rows)], load_sem.at[0]),
        pltpu.make_async_copy(speed_hbm, speed, load_sem.at[1]),
        pltpu.make_async_copy(prev_hbm, prev, load_sem.at[2]),
        pltpu.make_async_copy(adj_hbm, ext.at[STEPS, :, pl.ds(MARGIN, rows)], load_sem.at[3]),
        pltpu.make_async_copy(later_hbm, later, load_sem.at[4]),
    ]
    for load in loads:
        load.start()

    barrier = pltpu.get_barrier_semaphore()

    @pl.when(has_left)
    def _():
        pl.semaphore_signal(barrier, inc=1, device_id={"dom": left}, device_id_type=MESH)

    @pl.when(has_right)
    def _():
        pl.semaphore_signal(barrier, inc=1, device_id={"dom": right}, device_id_type=MESH)

    pl.semaphore_wait(barrier, has_left.astype(jnp.int32) + has_right.astype(jnp.int32))

    def halo_copies(slot, source):
        base = MARGIN if source is None else 0
        field = ext.at[slot] if source is None else source
        to_left = pltpu.make_async_remote_copy(
            src_ref=field.at[:, pl.ds(base, MARGIN)],
            dst_ref=ext.at[slot, :, pl.ds(high_start, MARGIN)],
            send_sem=send_sem.at[slot, 0],
            recv_sem=recv_sem.at[slot, 1],
            device_id={"dom": left},
            device_id_type=MESH,
        )
        to_right = pltpu.make_async_remote_copy(
            src_ref=field.at[:, pl.ds(base + rows - MARGIN, MARGIN)],
            dst_ref=ext.at[slot, :, pl.ds(0, MARGIN)],
            send_sem=send_sem.at[slot, 1],
            recv_sem=recv_sem.at[slot, 0],
            device_id={"dom": right},
            device_id_type=MESH,
        )
        return to_left, to_right

    copies = [
        halo_copies(slot, {0: now_hbm, STEPS: adj_hbm}.get(slot)) for slot in range(2 * STEPS)
    ]

    def send(slot):
        @pl.when(has_left)
        def _():
            copies[slot][0].start()

        @pl.when(has_right)
        def _():
            copies[slot][1].start()

    def receive(slot):
        @pl.when(has_left)
        def _():
            copies[slot][1].wait_recv()

        @pl.when(has_right)
        def _():
            copies[slot][0].wait_recv()

    send(0)
    send(STEPS)

    edge = jnp.zeros((2 * STEPS, shots, MARGIN, depth, width), jnp.float32)

    @pl.when(jnp.logical_not(has_left))
    def _():
        ext[pl.ds(0, 2 * STEPS), :, pl.ds(0, MARGIN)] = edge

    @pl.when(jnp.logical_not(has_right))
    def _():
        ext[pl.ds(0, 2 * STEPS), :, pl.ds(high_start, MARGIN)] = edge

    lanes = lax.broadcasted_iota(jnp.int32, (depth, width), 1)
    levels = lax.broadcasted_iota(jnp.int32, (depth, width), 0)

    span = chunk * depth
    receivers = record_cells.shape[1]
    first = here * (rows * depth)
    row_of = lambda cell: lax.div(cell, jnp.int32(width))
    lane_of = lambda cell: lax.rem(cell, jnp.int32(width))
    tile = (width, receivers)
    place = lax.broadcasted_iota(jnp.int32, tile, 0)
    for s in range(shots):
        cells = record_cells[s : s + 1, :]
        rec_rows = row_of(cells) - first
        table = jnp.where(
            place == STEPS,
            jnp.broadcast_to(rec_rows.astype(jnp.float32), tile),
            jnp.broadcast_to(lane_of(cells).astype(jnp.float32), tile),
        )
        for k in range(STEPS):
            table = jnp.where(place == k, jnp.broadcast_to(observed[s, k : k + 1, :], tile), table)
        columns[s] = jnp.transpose(table)
        rec_col = columns[s, :, STEPS : STEPS + 1].astype(jnp.int32)
        rec_lane = columns[s, :, STEPS + 1 : STEPS + 2].astype(jnp.int32)
        hot[s] = (lax.broadcasted_iota(jnp.int32, (receivers, width), 1) == rec_lane).astype(
            jnp.float32
        )
        count = src_cells.shape[1]
        padded = count + (-count) % 128
        order = lax.broadcasted_iota(jnp.int32, (padded, width), 0)
        across = lax.broadcasted_iota(jnp.int32, (padded, width), 1)
        along = lax.broadcasted_iota(jnp.int32, (1, padded), 1)
        tall = jnp.zeros((padded, width), jnp.float32)
        src_rows = jnp.full((1, padded), -1, jnp.int32)
        for j in range(count):
            cell = src_cells[s, j]
            sign = (2 * src_signs[s, j] - 1).astype(jnp.float32)
            tall = jnp.where((order == j) & (across == lane_of(cell)), sign, tall)
            src_rows = jnp.where(along == j, row_of(cell) - first, src_rows)
        tall = tall.astype(jnp.bfloat16)

        @pl.loop(0, chunks)
        def _(c):
            cell = lax.broadcasted_iota(jnp.int32, (receivers, span), 1) + c * span
            pick[s, c] = (cell == rec_col).astype(jnp.float32).astype(jnp.bfloat16)
            cell = lax.broadcasted_iota(jnp.int32, (span, receivers), 0) + c * span
            put[s, c] = (cell == rec_rows).astype(jnp.float32).astype(jnp.bfloat16)
            cell = lax.broadcasted_iota(jnp.int32, (span, padded), 0) + c * span
            wide = (cell == src_rows).astype(jnp.float32).astype(jnp.bfloat16)
            spots = jnp.dot(wide, tall, preferred_element_type=jnp.float32)
            spread_src[s, pl.ds(c * chunk, chunk)] = spots.reshape(chunk, depth, width)

    def laplacian(slot, s, x):
        middle = ext[slot, s, x + MARGIN]
        summed = 3.0 * COEFFS[0] * middle
        for r in range(1, MARGIN + 1):
            beside = ext[slot, s, x + MARGIN + r] + ext[slot, s, x + MARGIN - r]
            beside += jnp.where(levels < depth - r, pltpu.roll(middle, depth - r, 0), 0.0)
            beside += jnp.where(levels >= r, pltpu.roll(middle, r, 0), 0.0)
            beside += jnp.where(lanes < width - r, pltpu.roll(middle, width - r, 1), 0.0)
            beside += jnp.where(lanes >= r, pltpu.roll(middle, r, 1), 0.0)
            summed += COEFFS[r] * beside
        return middle, summed

    def forward(moment, first, last):
        @pl.loop(first, last, unroll=MARGIN)
        def _(x):
            squared = COURANT * speed[x] * speed[x]
            for s in range(shots):
                middle, summed = laplacian(moment, s, x)
                before = prev[s, x] if moment == 0 else ext[moment - 1, s, x + MARGIN]
                laps[moment, s, x] = summed
                slot = moment + 1 if moment + 1 < STEPS else 2 * STEPS
                ext[slot, s, x + MARGIN] = (
                    2.0 * middle - before + squared * summed + pulse[s, moment] * spread_src[s, x]
                )

    def backward(moment, first, last):
        slot = 2 * STEPS - moment

        @pl.loop(first, last, unroll=MARGIN)
        def _(x):
            squared = COURANT * speed[x] * speed[x]
            gathered = None
            for s in range(shots):
                middle, summed = laplacian(slot, s, x)
                after = later[s, x] if moment == STEPS else ext[slot - 1, s, x + MARGIN]
                earlier = 2.0 * middle - after + squared * summed + landed[moment - 1, s, x]
                if moment > 1:
                    ext[slot + 1, s, x + MARGIN] = earlier
                term = earlier * laps[moment - 1, s, x]
                gathered = term if gathered is None else gathered + term
            if moment < STEPS:
                gathered = gathered + total[x]
            if moment > 1:
                total[x] = gathered
            else:
                out[x] = 2.0 * COURANT * speed[x] * gathered

    def receivers_at(moment):
        slot = moment if moment < STEPS else 2 * STEPS
        for s in range(shots):
            @pl.loop(0, chunks)
            def _(c):
                block = ext[slot, s, pl.ds(MARGIN + c * chunk, chunk)].reshape(span, width)
                part = jnp.dot(pick[s, c], split_two(block), preferred_element_type=jnp.float32)

                @pl.when(c == 0)
                def _():
                    misfit[...] = part

                @pl.when(c > 0)
                def _():
                    misfit[...] += part

            found = misfit[:, :width] + misfit[:, width:]
            sample = jnp.sum(found * hot[s], axis=1, keepdims=True)
            miss = sample - columns[s, :, moment - 1 : moment]
            values = split_two(miss * hot[s])

            @pl.loop(0, chunks)
            def _(c):
                both = jnp.dot(put[s, c], values, preferred_element_type=jnp.float32)
                landed[moment - 1, s, pl.ds(c * chunk, chunk)] = (
                    both[:, :width] + both[:, width:]
                ).reshape(chunk, depth, width)

    for load in loads[:3]:
        load.wait()
    forward(0, MARGIN, rows - MARGIN)
    receive(0)
    forward(0, 0, MARGIN)
    forward(0, rows - MARGIN, rows)
    send(1)
    receivers_at(1)
    for moment in range(1, STEPS):
        receive(moment)
        forward(moment, 0, MARGIN)
        forward(moment, rows - MARGIN, rows)
        if moment + 1 < STEPS:
            send(moment + 1)
        forward(moment, MARGIN, rows - MARGIN)
        receivers_at(moment + 1)
    for load in loads[3:]:
        load.wait()
    for moment in range(STEPS, 0, -1):
        slot = 2 * STEPS - moment
        receive(slot)
        backward(moment, 0, MARGIN)
        backward(moment, rows - MARGIN, rows)
        if moment > 1:
            send(slot + 1)
        backward(moment, MARGIN, rows - MARGIN)
    for slot in range(2 * STEPS):
        @pl.when(has_left)
        def _():
            copies[slot][0].wait_send()

        @pl.when(has_right)
        def _():
            copies[slot][1].wait_send()


def shot_gradient(
    velocity, prev, now, later, adjoint, wavelet, source_cells, signs, record_cells, observed
):
    shots, rows, depth, width = now.shape
    receivers = record_cells.shape[1]
    chunk = 8
    span = chunk * depth
    hbm = pl.BlockSpec(memory_space=pl.ANY)
    vmem = pl.BlockSpec(memory_space=pltpu.VMEM)
    smem = pl.BlockSpec(memory_space=pltpu.SMEM)
    f32 = jnp.float32
    return pl.pallas_call(
        functools.partial(wave_kernel, lax.axis_size("dom")),
        out_shape=jax.ShapeDtypeStruct((rows, depth, width), f32),
        in_specs=[hbm] * 5 + [smem] * 3 + [vmem] * 2,
        out_specs=vmem,
        scratch_shapes=[
            pltpu.VMEM((2 * STEPS + 1, shots, rows + 2 * MARGIN, depth, width), f32),
            pltpu.VMEM((shots, rows, depth, width), f32),
            pltpu.VMEM((shots, rows, depth, width), f32),
            pltpu.VMEM((rows, depth, width), f32),
            pltpu.VMEM((STEPS, shots, rows, depth, width), f32),
            pltpu.VMEM((shots, rows, depth, width), f32),
            pltpu.VMEM((STEPS, shots, rows, depth, width), f32),
            pltpu.VMEM((shots, rows // chunk, receivers, span), jnp.bfloat16),
            pltpu.VMEM((shots, rows // chunk, span, receivers), jnp.bfloat16),
            pltpu.VMEM((shots, receivers, width), f32),
            pltpu.VMEM((shots, receivers, width), f32),
            pltpu.VMEM((receivers, 2 * width), f32),
            pltpu.VMEM((rows, depth, width), f32),
            pltpu.SemaphoreType.DMA((5,)),
            pltpu.SemaphoreType.DMA((2 * STEPS, 2)),
            pltpu.SemaphoreType.DMA((2 * STEPS, 2)),
        ],
        compiler_params=pltpu.CompilerParams(
            collective_id=0, has_side_effects=True, vmem_limit_bytes=56 * 1024 * 1024
        ),
    )(
        now,
        adjoint,
        prev,
        later,
        velocity,
        wavelet,
        source_cells,
        signs,
        record_cells,
        observed,
    )


def cosine_basis(length):
    wave_index = jnp.arange(length, dtype=jnp.int32)[:, None]
    position = jnp.arange(length, dtype=jnp.int32)[None, :]
    phase = wave_index * (2 * position + 1) % (4 * length)
    angle = math.pi / (2.0 * length) * phase.astype(jnp.float32)
    factor = jnp.where(wave_index == 0, math.sqrt(1.0 / length), math.sqrt(2.0 / length)).astype(
        jnp.float32
    )
    return factor * jnp.cos(angle)


def prior_gain(length, cutoff):
    scaled = jnp.arange(length, dtype=jnp.float32) / float(cutoff)
    return 1.0 / jnp.sqrt(1.0 + scaled)


def precondition(gradient, noise_cols, rate):
    length = gradient.shape[0]
    basis = cosine_basis(length)
    spectrum = prior_gain(length, length // 32)[:, None]
    highest = lax.Precision.HIGHEST
    grad_hat = jnp.dot(basis, gradient.reshape(length, -1), precision=highest)
    noise_hat = jnp.dot(basis, noise_cols.reshape(length, -1), precision=highest)
    weights = spectrum * (-0.5 * rate * spectrum * grad_hat + jnp.sqrt(rate) * noise_hat)
    update = lax.dot_general(basis, weights, (((0,), (0,)), ((), ())), precision=highest)
    return update.reshape(gradient.shape)


def shared_kernel(
    shots,
    doms,
    partial,
    noise,
    basis,
    basis_t,
    gain,
    step_size,
    out,
    folded,
    noise_fold,
    sums,
    own,
    noise_lines,
    grad_lines,
    update,
    returned,
    send_sem,
    recv_sem,
    shot_send,
    shot_recv,
):
    depth, rows, width = shots * folded.shape[1], folded.shape[2], folded.shape[3]
    fold = folded.shape[1]
    lot = fold // doms
    lane_share = width // shots
    me = lax.axis_index("shot")
    here = lax.axis_index("dom")
    dom_peer = [lax.rem(here + o, doms) for o in range(doms)]
    shot_peer = [lax.rem(me + o, shots) for o in range(shots)]

    barrier = pltpu.get_barrier_semaphore()
    for o in range(1, doms):
        pl.semaphore_signal(barrier, inc=1, device_id={"dom": dom_peer[o]}, device_id_type=MESH)
    for o in range(1, shots):
        pl.semaphore_signal(barrier, inc=1, device_id={"shot": shot_peer[o]}, device_id_type=MESH)

    group = lax.broadcasted_iota(jnp.int32, (rows, width), 1) // lane_share

    def fold_lanes(source, target):
        @pl.loop(0, fold)
        def _(level):
            slabs = [
                source[pl.ds(block * fold + level, rows, stride=depth), :]
                for block in range(shots)
            ]
            for share in range(shots):
                merged = None
                for block in range(shots):
                    shift = (block - share) * lane_share % width
                    turned = pltpu.roll(slabs[block], shift, 1) if shift else slabs[block]
                    merged = turned if merged is None else jnp.where(group == block, turned, merged)
                target[share, level] = merged

    def exchange(phase, source_of, target):
        moves = []
        for o in range(1, doms):
            moves.append(
                pltpu.make_async_remote_copy(
                    src_ref=source_of(dom_peer[o]),
                    dst_ref=target.at[here],
                    send_sem=send_sem.at[phase, o],
                    recv_sem=recv_sem.at[phase, o],
                    device_id={"dom": dom_peer[o]},
                    device_id_type=MESH,
                )
            )
        return moves

    fold_lanes(partial, folded)
    pl.semaphore_wait(barrier, doms + shots - 2)
    sharing = []
    for o in range(1, shots):
        move = pltpu.make_async_remote_copy(
            src_ref=folded.at[shot_peer[o]],
            dst_ref=sums.at[o],
            send_sem=shot_send.at[o],
            recv_sem=shot_recv.at[o],
            device_id={"shot": shot_peer[o]},
            device_id_type=MESH,
        )
        move.start()
        sharing.append(move)
    fold_lanes(noise, noise_fold)
    noise_moves = exchange(0, lambda d: noise_fold.at[me, pl.ds(d * lot, lot)], noise_lines)
    for move in noise_moves:
        move.start()
    noise_lines[here] = noise_fold[me, pl.ds(here * lot, lot)]
    for move in noise_moves:
        move.wait_recv()
    rate = step_size[0]
    highest = lax.Precision.HIGHEST
    lines = doms * rows
    noise_hats = [
        jnp.dot(
            basis[...],
            noise_lines[:, i].reshape(lines, width),
            precision=highest,
            preferred_element_type=jnp.float32,
        )
        for i in range(lot)
    ]
    root = jnp.sqrt(jnp.full((1, 1), rate, jnp.float32))
    for move in sharing:
        move.wait_recv()
    gathered = folded[me]
    for o in range(1, shots):
        gathered = gathered + sums[o]
    own[...] = gathered
    grad_moves = exchange(1, lambda d: own.at[pl.ds(d * lot, lot)], grad_lines)
    for move in grad_moves:
        move.start()
    grad_lines[here] = own[pl.ds(here * lot, lot)]
    for move in grad_moves:
        move.wait_recv()
    for i in range(lot):
        grad_hat = jnp.dot(
            basis[...],
            grad_lines[:, i].reshape(lines, width),
            precision=highest,
            preferred_element_type=jnp.float32,
        )
        weights = gain[...] * (-0.5 * rate * gain[...] * grad_hat + root * noise_hats[i])
        update[:, i] = jnp.dot(
            basis_t[...], weights, precision=highest, preferred_element_type=jnp.float32
        ).reshape(doms, rows, width)
    back_moves = exchange(2, lambda d: update.at[d], returned)
    for move in back_moves:
        move.start()
    returned[here] = update[here]
    for move in back_moves:
        move.wait_recv()
    for d in range(doms):
        for i in range(lot):
            line = returned[d, i]
            for block in range(shots):
                shift = -block * lane_share % width
                turned = pltpu.roll(line, shift, 1) if shift else line
                out[pl.ds(block * fold + d * lot + i, rows, stride=depth), :] = turned
    for move in sharing + noise_moves + grad_moves + back_moves:
        move.wait_send()


def shared_update(partial_value, noise_field, step_size):
    rows, depth, width = partial_value.shape
    shots, doms = lax.axis_size("shot"), lax.axis_size("dom")
    length = rows * doms
    fold = depth // shots
    lot = fold // doms
    wave = np.arange(length)[:, None]
    phase = wave * (2 * np.arange(length)[None, :] + 1) % (4 * length)
    factor = np.where(wave == 0, math.sqrt(1.0 / length), math.sqrt(2.0 / length))
    basis = (factor * np.cos(math.pi / (2.0 * length) * phase)).astype(np.float32)
    gain = (1.0 / np.sqrt(1.0 + wave / (length // 32))).astype(np.float32)
    f32 = jnp.float32
    vmem = pl.BlockSpec(memory_space=pltpu.VMEM)
    smem = pl.BlockSpec(memory_space=pltpu.SMEM)
    result = pl.pallas_call(
        functools.partial(shared_kernel, shots, doms),
        out_shape=jax.ShapeDtypeStruct((rows * depth, width), f32),
        in_specs=[vmem] * 5 + [smem],
        out_specs=vmem,
        scratch_shapes=[
            pltpu.VMEM((shots, fold, rows, width), f32),
            pltpu.VMEM((shots, fold, rows, width), f32),
            pltpu.VMEM((shots, fold, rows, width), f32),
            pltpu.VMEM((fold, rows, width), f32),
            pltpu.VMEM((doms, lot, rows, width), f32),
            pltpu.VMEM((doms, lot, rows, width), f32),
            pltpu.VMEM((doms, lot, rows, width), f32),
            pltpu.VMEM((doms, lot, rows, width), f32),
            pltpu.SemaphoreType.DMA((3, doms)),
            pltpu.SemaphoreType.DMA((3, doms)),
            pltpu.SemaphoreType.DMA((shots,)),
            pltpu.SemaphoreType.DMA((shots,)),
        ],
        compiler_params=pltpu.CompilerParams(
            collective_id=1, has_side_effects=True, vmem_limit_bytes=32 * 1024 * 1024
        ),
    )(
        partial_value.reshape(rows * depth, width),
        noise_field.reshape(rows * depth, width),
        jnp.asarray(basis),
        jnp.asarray(np.ascontiguousarray(basis.T)),
        jnp.asarray(gain),
        step_size,
    )
    return result.reshape(rows, depth, width)[:, :, : width // shots]


def body(
    velocity,
    noise_field,
    step_size,
    field_prev,
    field_now,
    adjoint_next,
    adjoint_now,
    wavelet,
    source_cells,
    source_signs,
    record_cells,
    observed,
):
    partial_value = shot_gradient(
        velocity,
        field_prev,
        field_now,
        adjoint_next,
        adjoint_now,
        wavelet,
        source_cells,
        source_signs,
        record_cells,
        observed,
    )
    rate = step_size[0]
    shot_rows = velocity.shape[2] // lax.axis_size("shot")
    start = lax.axis_index("shot") * shot_rows
    if velocity.shape[1] % (lax.axis_size("shot") * lax.axis_size("dom")) == 0:
        moved = shared_update(partial_value, noise_field, step_size)
        return lax.dynamic_slice_in_dim(velocity, start, shot_rows, 2) + moved
    share = lax.psum_scatter(partial_value, "shot", scatter_dimension=2, tiled=True)
    noise_part = lax.dynamic_slice_in_dim(noise_field, start, shot_rows, 2)
    grad_cols, noise_cols = (
        lax.all_to_all(share, "dom", split_axis=2, concat_axis=0, tiled=True),
        lax.all_to_all(noise_part, "dom", split_axis=2, concat_axis=0, tiled=True),
    )
    update = precondition(grad_cols, noise_cols, rate)
    returned = lax.all_to_all(update, "dom", split_axis=0, concat_axis=2, tiled=True)
    result = lax.dynamic_slice_in_dim(velocity, start, shot_rows, 2) + returned
    return result


def solution(mesh):
    placed = (
        P("dom", None, None),
        P("dom", None, None),
        P(),
        P("shot", "dom", None, None),
        P("shot", "dom", None, None),
        P("shot", "dom", None, None),
        P("shot", "dom", None, None),
        P("shot", None),
        P("shot", None),
        P("shot", None),
        P("shot", None),
        P("shot", None, None),
    )
    return jax.shard_map(
        body, mesh=mesh, in_specs=placed, out_specs=P("dom", None, "shot"), check_vma=False
    )
```

```python
import functools
import math

import jax
import jax.numpy as jnp
import numpy as np
from jax import lax
from jax.experimental import pallas as pl
from jax.experimental.pallas import tpu as pltpu
from jax.sharding import PartitionSpec as P

STEPS = 4


COEFFS = (-205.0 / 72.0, 8.0 / 5.0, -1.0 / 5.0, 8.0 / 315.0, -1.0 / 560.0)
COURANT = 0.02


MARGIN = 4
MESH = pl.DeviceIdType.MESH


def split_two(value):
    high = value.astype(jnp.bfloat16)
    low = (value - high.astype(jnp.float32)).astype(jnp.bfloat16)
    return jnp.concatenate([high, low], axis=-1)


def wave_kernel(
    doms,
    now_hbm,
    adj_hbm,
    prev_hbm,
    later_hbm,
    speed_hbm,
    pulse,
    src_cells,
    src_signs,
    record_cells,
    observed,
    out,
    ext,
    prev,
    later,
    speed,
    laps,
    spread_src,
    landed,
    pick,
    put,
    hot,
    columns,
    misfit,
    total,
    load_sem,
    send_sem,
    recv_sem,
):
    shots, rows, depth, width = prev.shape
    here = lax.axis_index("dom")
    left = jnp.maximum(here - 1, 0)
    right = jnp.minimum(here + 1, doms - 1)
    has_left = here > 0
    has_right = here < doms - 1
    chunk = 8
    chunks = rows // chunk
    high_start = rows + MARGIN

    loads = [
        pltpu.make_async_copy(now_hbm, ext.at[0, :, pl.ds(MARGIN, rows)], load_sem.at[0]),
        pltpu.make_async_copy(speed_hbm, speed, load_sem.at[1]),
        pltpu.make_async_copy(prev_hbm, prev, load_sem.at[2]),
        pltpu.make_async_copy(adj_hbm, ext.at[STEPS, :, pl.ds(MARGIN, rows)], load_sem.at[3]),
        pltpu.make_async_copy(later_hbm, later, load_sem.at[4]),
    ]
    for load in loads:
        load.start()

    barrier = pltpu.get_barrier_semaphore()

    @pl.when(has_left)
    def _():
        pl.semaphore_signal(barrier, inc=1, device_id={"dom": left}, device_id_type=MESH)

    @pl.when(has_right)
    def _():
        pl.semaphore_signal(barrier, inc=1, device_id={"dom": right}, device_id_type=MESH)

    pl.semaphore_wait(barrier, has_left.astype(jnp.int32) + has_right.astype(jnp.int32))

    def halo_copies(slot, source):
        base = MARGIN if source is None else 0
        field = ext.at[slot] if source is None else source
        to_left = pltpu.make_async_remote_copy(
            src_ref=field.at[:, pl.ds(base, MARGIN)],
            dst_ref=ext.at[slot, :, pl.ds(high_start, MARGIN)],
            send_sem=send_sem.at[slot, 0],
            recv_sem=recv_sem.at[slot, 1],
            device_id={"dom": left},
            device_id_type=MESH,
        )
        to_right = pltpu.make_async_remote_copy(
            src_ref=field.at[:, pl.ds(base + rows - MARGIN, MARGIN)],
            dst_ref=ext.at[slot, :, pl.ds(0, MARGIN)],
            send_sem=send_sem.at[slot, 1],
            recv_sem=recv_sem.at[slot, 0],
            device_id={"dom": right},
            device_id_type=MESH,
        )
        return to_left, to_right

    copies = [
        halo_copies(slot, {0: now_hbm, STEPS: adj_hbm}.get(slot)) for slot in range(2 * STEPS)
    ]

    def send(slot):
        @pl.when(has_left)
        def _():
            copies[slot][0].start()

        @pl.when(has_right)
        def _():
            copies[slot][1].start()

    def receive(slot):
        @pl.when(has_left)
        def _():
            copies[slot][1].wait_recv()

        @pl.when(has_right)
        def _():
            copies[slot][0].wait_recv()

    send(0)
    send(STEPS)

    edge = jnp.zeros((2 * STEPS, shots, MARGIN, depth, width), jnp.float32)

    @pl.when(jnp.logical_not(has_left))
    def _():
        ext[pl.ds(0, 2 * STEPS), :, pl.ds(0, MARGIN)] = edge

    @pl.when(jnp.logical_not(has_right))
    def _():
        ext[pl.ds(0, 2 * STEPS), :, pl.ds(high_start, MARGIN)] = edge

    lanes = lax.broadcasted_iota(jnp.int32, (depth, width), 1)
    nothing = jnp.zeros((MARGIN, width), jnp.float32)

    span = chunk * depth
    receivers = record_cells.shape[1]
    first = here * (rows * depth)
    row_of = lambda cell: lax.div(cell, jnp.int32(width))
    lane_of = lambda cell: lax.rem(cell, jnp.int32(width))
    tile = (width, receivers)
    place = lax.broadcasted_iota(jnp.int32, tile, 0)
    for s in range(shots):
        cells = record_cells[s : s + 1, :]
        rec_rows = row_of(cells) - first
        table = jnp.where(
            place == STEPS,
            jnp.broadcast_to(rec_rows.astype(jnp.float32), tile),
            jnp.broadcast_to(lane_of(cells).astype(jnp.float32), tile),
        )
        for k in range(STEPS):
            table = jnp.where(place == k, jnp.broadcast_to(observed[s, k : k + 1, :], tile), table)
        columns[s] = jnp.transpose(table)
        rec_col = columns[s, :, STEPS : STEPS + 1].astype(jnp.int32)
        rec_lane = columns[s, :, STEPS + 1 : STEPS + 2].astype(jnp.int32)
        hot[s] = (lax.broadcasted_iota(jnp.int32, (receivers, width), 1) == rec_lane).astype(
            jnp.float32
        )
        count = src_cells.shape[1]
        padded = count + (-count) % 128
        order = lax.broadcasted_iota(jnp.int32, (padded, width), 0)
        across = lax.broadcasted_iota(jnp.int32, (padded, width), 1)
        along = lax.broadcasted_iota(jnp.int32, (1, padded), 1)
        tall = jnp.zeros((padded, width), jnp.float32)
        src_rows = jnp.full((1, padded), -1, jnp.int32)
        for j in range(count):
            cell = src_cells[s, j]
            sign = (2 * src_signs[s, j] - 1).astype(jnp.float32)
            tall = jnp.where((order == j) & (across == lane_of(cell)), sign, tall)
            src_rows = jnp.where(along == j, row_of(cell) - first, src_rows)
        tall = tall.astype(jnp.bfloat16)

        @pl.loop(0, chunks)
        def _(c):
            cell = lax.broadcasted_iota(jnp.int32, (receivers, span), 1) + c * span
            pick[s, c] = (cell == rec_col).astype(jnp.float32).astype(jnp.bfloat16)
            cell = lax.broadcasted_iota(jnp.int32, (span, receivers), 0) + c * span
            put[s, c] = (cell == rec_rows).astype(jnp.float32).astype(jnp.bfloat16)
            cell = lax.broadcasted_iota(jnp.int32, (span, padded), 0) + c * span
            wide = (cell == src_rows).astype(jnp.float32).astype(jnp.bfloat16)
            spots = jnp.dot(wide, tall, preferred_element_type=jnp.float32)
            spread_src[s, pl.ds(c * chunk, chunk)] = spots.reshape(chunk, depth, width)

    def laplacian(slot, s, x):
        middle = ext[slot, s, x + MARGIN]
        summed = 3.0 * COEFFS[0] * middle
        for r in range(1, MARGIN + 1):
            beside = ext[slot, s, x + MARGIN + r] + ext[slot, s, x + MARGIN - r]
            beside += jnp.concatenate([middle[r:], nothing[:r]], axis=0)
            beside += jnp.concatenate([nothing[:r], middle[: depth - r]], axis=0)
            beside += jnp.where(lanes < width - r, pltpu.roll(middle, width - r, 1), 0.0)
            beside += jnp.where(lanes >= r, pltpu.roll(middle, r, 1), 0.0)
            summed += COEFFS[r] * beside
        return middle, summed

    def forward(moment, first, last):
        @pl.loop(first, last, unroll=MARGIN)
        def _(x):
            squared = COURANT * speed[x] * speed[x]
            for s in range(shots):
                middle, summed = laplacian(moment, s, x)
                before = prev[s, x] if moment == 0 else ext[moment - 1, s, x + MARGIN]
                laps[moment, s, x] = summed
                slot = moment + 1 if moment + 1 < STEPS else 2 * STEPS
                ext[slot, s, x + MARGIN] = (
                    2.0 * middle - before + squared * summed + pulse[s, moment] * spread_src[s, x]
                )

    def backward(moment, first, last):
        slot = 2 * STEPS - moment

        @pl.loop(first, last, unroll=MARGIN)
        def _(x):
            squared = COURANT * speed[x] * speed[x]
            gathered = None
            for s in range(shots):
                middle, summed = laplacian(slot, s, x)
                after = later[s, x] if moment == STEPS else ext[slot - 1, s, x + MARGIN]
                earlier = 2.0 * middle - after + squared * summed + landed[moment - 1, s, x]
                if moment > 1:
                    ext[slot + 1, s, x + MARGIN] = earlier
                term = earlier * laps[moment - 1, s, x]
                gathered = term if gathered is None else gathered + term
            if moment < STEPS:
                gathered = gathered + total[x]
            if moment > 1:
                total[x] = gathered
            else:
                out[x] = 2.0 * COURANT * speed[x] * gathered

    def receivers_at(moment):
        slot = moment if moment < STEPS else 2 * STEPS
        for s in range(shots):
            @pl.loop(0, chunks)
            def _(c):
                block = ext[slot, s, pl.ds(MARGIN + c * chunk, chunk)].reshape(span, width)
                part = jnp.dot(pick[s, c], split_two(block), preferred_element_type=jnp.float32)

                @pl.when(c == 0)
                def _():
                    misfit[...] = part

                @pl.when(c > 0)
                def _():
                    misfit[...] += part

            found = misfit[:, :width] + misfit[:, width:]
            sample = jnp.sum(found * hot[s], axis=1, keepdims=True)
            miss = sample - columns[s, :, moment - 1 : moment]
            values = split_two(miss * hot[s])

            @pl.loop(0, chunks)
            def _(c):
                both = jnp.dot(put[s, c], values, preferred_element_type=jnp.float32)
                landed[moment - 1, s, pl.ds(c * chunk, chunk)] = (
                    both[:, :width] + both[:, width:]
                ).reshape(chunk, depth, width)

    for load in loads[:3]:
        load.wait()
    forward(0, MARGIN, rows - MARGIN)
    receive(0)
    forward(0, 0, MARGIN)
    forward(0, rows - MARGIN, rows)
    send(1)
    receivers_at(1)
    for moment in range(1, STEPS):
        receive(moment)
        forward(moment, 0, MARGIN)
        forward(moment, rows - MARGIN, rows)
        if moment + 1 < STEPS:
            send(moment + 1)
        forward(moment, MARGIN, rows - MARGIN)
        receivers_at(moment + 1)
    for load in loads[3:]:
        load.wait()
    for moment in range(STEPS, 0, -1):
        slot = 2 * STEPS - moment
        receive(slot)
        backward(moment, 0, MARGIN)
        backward(moment, rows - MARGIN, rows)
        if moment > 1:
            send(slot + 1)
        backward(moment, MARGIN, rows - MARGIN)
    for slot in range(2 * STEPS):
        @pl.when(has_left)
        def _():
            copies[slot][0].wait_send()

        @pl.when(has_right)
        def _():
            copies[slot][1].wait_send()


def shot_gradient(
    velocity, prev, now, later, adjoint, wavelet, source_cells, signs, record_cells, observed
):
    shots, rows, depth, width = now.shape
    receivers = record_cells.shape[1]
    chunk = 8
    span = chunk * depth
    hbm = pl.BlockSpec(memory_space=pl.ANY)
    vmem = pl.BlockSpec(memory_space=pltpu.VMEM)
    smem = pl.BlockSpec(memory_space=pltpu.SMEM)
    f32 = jnp.float32
    return pl.pallas_call(
        functools.partial(wave_kernel, lax.axis_size("dom")),
        out_shape=jax.ShapeDtypeStruct((rows, depth, width), f32),
        in_specs=[hbm] * 5 + [smem] * 3 + [vmem] * 2,
        out_specs=vmem,
        scratch_shapes=[
            pltpu.VMEM((2 * STEPS + 1, shots, rows + 2 * MARGIN, depth, width), f32),
            pltpu.VMEM((shots, rows, depth, width), f32),
            pltpu.VMEM((shots, rows, depth, width), f32),
            pltpu.VMEM((rows, depth, width), f32),
            pltpu.VMEM((STEPS, shots, rows, depth, width), f32),
            pltpu.VMEM((shots, rows, depth, width), f32),
            pltpu.VMEM((STEPS, shots, rows, depth, width), f32),
            pltpu.VMEM((shots, rows // chunk, receivers, span), jnp.bfloat16),
            pltpu.VMEM((shots, rows // chunk, span, receivers), jnp.bfloat16),
            pltpu.VMEM((shots, receivers, width), f32),
            pltpu.VMEM((shots, receivers, width), f32),
            pltpu.VMEM((receivers, 2 * width), f32),
            pltpu.VMEM((rows, depth, width), f32),
            pltpu.SemaphoreType.DMA((5,)),
            pltpu.SemaphoreType.DMA((2 * STEPS, 2)),
            pltpu.SemaphoreType.DMA((2 * STEPS, 2)),
        ],
        compiler_params=pltpu.CompilerParams(
            collective_id=0, has_side_effects=True, vmem_limit_bytes=56 * 1024 * 1024
        ),
    )(
        now,
        adjoint,
        prev,
        later,
        velocity,
        wavelet,
        source_cells,
        signs,
        record_cells,
        observed,
    )


def cosine_basis(length):
    wave_index = jnp.arange(length, dtype=jnp.int32)[:, None]
    position = jnp.arange(length, dtype=jnp.int32)[None, :]
    phase = wave_index * (2 * position + 1) % (4 * length)
    angle = math.pi / (2.0 * length) * phase.astype(jnp.float32)
    factor = jnp.where(wave_index == 0, math.sqrt(1.0 / length), math.sqrt(2.0 / length)).astype(
        jnp.float32
    )
    return factor * jnp.cos(angle)


def prior_gain(length, cutoff):
    scaled = jnp.arange(length, dtype=jnp.float32) / float(cutoff)
    return 1.0 / jnp.sqrt(1.0 + scaled)


def precondition(gradient, noise_cols, rate):
    length = gradient.shape[0]
    basis = cosine_basis(length)
    spectrum = prior_gain(length, length // 32)[:, None]
    highest = lax.Precision.HIGHEST
    grad_hat = jnp.dot(basis, gradient.reshape(length, -1), precision=highest)
    noise_hat = jnp.dot(basis, noise_cols.reshape(length, -1), precision=highest)
    weights = spectrum * (-0.5 * rate * spectrum * grad_hat + jnp.sqrt(rate) * noise_hat)
    update = lax.dot_general(basis, weights, (((0,), (0,)), ((), ())), precision=highest)
    return update.reshape(gradient.shape)


def shared_kernel(
    shots,
    doms,
    partial,
    noise,
    basis,
    basis_t,
    gain,
    step_size,
    out,
    folded,
    noise_fold,
    sums,
    own,
    noise_lines,
    grad_lines,
    update,
    returned,
    send_sem,
    recv_sem,
    shot_send,
    shot_recv,
):
    depth, rows, width = shots * folded.shape[1], folded.shape[2], folded.shape[3]
    fold = folded.shape[1]
    lot = fold // doms
    lane_share = width // shots
    me = lax.axis_index("shot")
    here = lax.axis_index("dom")
    dom_peer = [lax.rem(here + o, doms) for o in range(doms)]
    shot_peer = [lax.rem(me + o, shots) for o in range(shots)]

    barrier = pltpu.get_barrier_semaphore()
    for o in range(1, doms):
        pl.semaphore_signal(barrier, inc=1, device_id={"dom": dom_peer[o]}, device_id_type=MESH)
    for o in range(1, shots):
        pl.semaphore_signal(barrier, inc=1, device_id={"shot": shot_peer[o]}, device_id_type=MESH)

    group = lax.broadcasted_iota(jnp.int32, (rows, width), 1) // lane_share

    def fold_lanes(source, target):
        @pl.loop(0, fold)
        def _(level):
            slabs = [
                source[pl.ds(block * fold + level, rows, stride=depth), :]
                for block in range(shots)
            ]
            for share in range(shots):
                merged = None
                for block in range(shots):
                    shift = (block - share) * lane_share % width
                    turned = pltpu.roll(slabs[block], shift, 1) if shift else slabs[block]
                    merged = turned if merged is None else jnp.where(group == block, turned, merged)
                target[share, level] = merged

    def exchange(phase, source_of, target):
        moves = []
        for o in range(1, doms):
            moves.append(
                pltpu.make_async_remote_copy(
                    src_ref=source_of(dom_peer[o]),
                    dst_ref=target.at[here],
                    send_sem=send_sem.at[phase, o],
                    recv_sem=recv_sem.at[phase, o],
                    device_id={"dom": dom_peer[o]},
                    device_id_type=MESH,
                )
            )
        return moves

    fold_lanes(partial, folded)
    pl.semaphore_wait(barrier, doms + shots - 2)
    sharing = []
    for o in range(1, shots):
        move = pltpu.make_async_remote_copy(
            src_ref=folded.at[shot_peer[o]],
            dst_ref=sums.at[o],
            send_sem=shot_send.at[o],
            recv_sem=shot_recv.at[o],
            device_id={"shot": shot_peer[o]},
            device_id_type=MESH,
        )
        move.start()
        sharing.append(move)
    fold_lanes(noise, noise_fold)
    noise_moves = exchange(0, lambda d: noise_fold.at[me, pl.ds(d * lot, lot)], noise_lines)
    for move in noise_moves:
        move.start()
    noise_lines[here] = noise_fold[me, pl.ds(here * lot, lot)]
    for move in noise_moves:
        move.wait_recv()
    rate = step_size[0]
    highest = lax.Precision.HIGHEST
    lines = doms * rows
    noise_hats = [
        jnp.dot(
            basis[...],
            noise_lines[:, i].reshape(lines, width),
            precision=highest,
            preferred_element_type=jnp.float32,
        )
        for i in range(lot)
    ]
    root = jnp.sqrt(jnp.full((1, 1), rate, jnp.float32))
    for move in sharing:
        move.wait_recv()
    gathered = folded[me]
    for o in range(1, shots):
        gathered = gathered + sums[o]
    own[...] = gathered
    grad_moves = exchange(1, lambda d: own.at[pl.ds(d * lot, lot)], grad_lines)
    for move in grad_moves:
        move.start()
    grad_lines[here] = own[pl.ds(here * lot, lot)]
    for move in grad_moves:
        move.wait_recv()
    for i in range(lot):
        grad_hat = jnp.dot(
            basis[...],
            grad_lines[:, i].reshape(lines, width),
            precision=highest,
            preferred_element_type=jnp.float32,
        )
        weights = gain[...] * (-0.5 * rate * gain[...] * grad_hat + root * noise_hats[i])
        update[:, i] = jnp.dot(
            basis_t[...], weights, precision=highest, preferred_element_type=jnp.float32
        ).reshape(doms, rows, width)
    back_moves = exchange(2, lambda d: update.at[d], returned)
    for move in back_moves:
        move.start()
    returned[here] = update[here]
    for move in back_moves:
        move.wait_recv()
    for d in range(doms):
        for i in range(lot):
            line = returned[d, i]
            for block in range(shots):
                shift = -block * lane_share % width
                turned = pltpu.roll(line, shift, 1) if shift else line
                out[pl.ds(block * fold + d * lot + i, rows, stride=depth), :] = turned
    for move in sharing + noise_moves + grad_moves + back_moves:
        move.wait_send()


def shared_update(partial_value, noise_field, step_size):
    rows, depth, width = partial_value.shape
    shots, doms = lax.axis_size("shot"), lax.axis_size("dom")
    length = rows * doms
    fold = depth // shots
    lot = fold // doms
    wave = np.arange(length)[:, None]
    phase = wave * (2 * np.arange(length)[None, :] + 1) % (4 * length)
    factor = np.where(wave == 0, math.sqrt(1.0 / length), math.sqrt(2.0 / length))
    basis = (factor * np.cos(math.pi / (2.0 * length) * phase)).astype(np.float32)
    gain = (1.0 / np.sqrt(1.0 + wave / (length // 32))).astype(np.float32)
    f32 = jnp.float32
    vmem = pl.BlockSpec(memory_space=pltpu.VMEM)
    smem = pl.BlockSpec(memory_space=pltpu.SMEM)
    result = pl.pallas_call(
        functools.partial(shared_kernel, shots, doms),
        out_shape=jax.ShapeDtypeStruct((rows * depth, width), f32),
        in_specs=[vmem] * 5 + [smem],
        out_specs=vmem,
        scratch_shapes=[
            pltpu.VMEM((shots, fold, rows, width), f32),
            pltpu.VMEM((shots, fold, rows, width), f32),
            pltpu.VMEM((shots, fold, rows, width), f32),
            pltpu.VMEM((fold, rows, width), f32),
            pltpu.VMEM((doms, lot, rows, width), f32),
            pltpu.VMEM((doms, lot, rows, width), f32),
            pltpu.VMEM((doms, lot, rows, width), f32),
            pltpu.VMEM((doms, lot, rows, width), f32),
            pltpu.SemaphoreType.DMA((3, doms)),
            pltpu.SemaphoreType.DMA((3, doms)),
            pltpu.SemaphoreType.DMA((shots,)),
            pltpu.SemaphoreType.DMA((shots,)),
        ],
        compiler_params=pltpu.CompilerParams(
            collective_id=1, has_side_effects=True, vmem_limit_bytes=32 * 1024 * 1024
        ),
    )(
        partial_value.reshape(rows * depth, width),
        noise_field.reshape(rows * depth, width),
        jnp.asarray(basis),
        jnp.asarray(np.ascontiguousarray(basis.T)),
        jnp.asarray(gain),
        step_size,
    )
    return result.reshape(rows, depth, width)[:, :, : width // shots]


def body(
    velocity,
    noise_field,
    step_size,
    field_prev,
    field_now,
    adjoint_next,
    adjoint_now,
    wavelet,
    source_cells,
    source_signs,
    record_cells,
    observed,
):
    partial_value = shot_gradient(
        velocity,
        field_prev,
        field_now,
        adjoint_next,
        adjoint_now,
        wavelet,
        source_cells,
        source_signs,
        record_cells,
        observed,
    )
    rate = step_size[0]
    shot_rows = velocity.shape[2] // lax.axis_size("shot")
    start = lax.axis_index("shot") * shot_rows
    if velocity.shape[1] % (lax.axis_size("shot") * lax.axis_size("dom")) == 0:
        moved = shared_update(partial_value, noise_field, step_size)
        return lax.dynamic_slice_in_dim(velocity, start, shot_rows, 2) + moved
    share = lax.psum_scatter(partial_value, "shot", scatter_dimension=2, tiled=True)
    noise_part = lax.dynamic_slice_in_dim(noise_field, start, shot_rows, 2)
    grad_cols, noise_cols = (
        lax.all_to_all(share, "dom", split_axis=2, concat_axis=0, tiled=True),
        lax.all_to_all(noise_part, "dom", split_axis=2, concat_axis=0, tiled=True),
    )
    update = precondition(grad_cols, noise_cols, rate)
    returned = lax.all_to_all(update, "dom", split_axis=0, concat_axis=2, tiled=True)
    result = lax.dynamic_slice_in_dim(velocity, start, shot_rows, 2) + returned
    return result


def solution(mesh):
    placed = (
        P("dom", None, None),
        P("dom", None, None),
        P(),
        P("shot", "dom", None, None),
        P("shot", "dom", None, None),
        P("shot", "dom", None, None),
        P("shot", "dom", None, None),
        P("shot", None),
        P("shot", None),
        P("shot", None),
        P("shot", None),
        P("shot", None, None),
    )
    return jax.shard_map(
        body, mesh=mesh, in_specs=placed, out_specs=P("dom", None, "shot"), check_vma=False
    )
```
